256 devices in a mesh: seg: 8 (over y, core), ep: 32 (over z, x).
Axes of the slice: x: 4, y: 4, z: 8, core: 2. Of those that a mesh axis runs over, the one named last changes fastest.
Arguments:
- queries: bfloat16 [16384, 8192], P(('seg', 'ep')), may hold values from -6 to 6
- keys: bfloat16 [16384, 8192], P(('seg', 'ep')), may hold values from -1.25 to 1.25
- values: bfloat16 [16384, 8192], P(('seg', 'ep')), may hold values from -54 to 54
- log_decay: float32 [16384, 64], P('seg', 'ep'), may hold values from -1 to 0
- out_gain: float32 [8192], replicated, may hold values from 0.1 to 1.9
- out_proj: bfloat16 [8192, 6144], P('ep', 'seg'), may hold values from -0.0625 to 0.0625
- experts: int32 [2048, 2], P(('seg', 'ep')), may hold values from 0 to 15, all different within a row; in each aligned block of 8 rows (0 to 7, 8 to 15, ...) at most 2 rows name the same one
- gates: float32 [2048, 2], P(('seg', 'ep')), may hold values from 0.2 to 1
- up_weight: bfloat16 [32, 6144, 2304], P('ep', None, 'seg'), may hold values from -0.078125 to 0.078125
- down_weight: bfloat16 [32, 2304, 6144], P('ep', 'seg'), may hold values from -0.09375 to 0.09375
Outputs:
- attn_out: bfloat16 [16384, 8192], P(('seg', 'ep'))
- moe_out: bfloat16 [2048, 6144], P(('seg', 'ep'))
The draws below stay inside these ranges and needn't reach their ends.
Inputs may be any that keep to these rules, and one draw needn't show every extreme that they name: Each row names two different experts. The 8 rows of one device name any one expert at most 2 times, and in some devices one expert exactly 2 times.
All inputs are finite; a program needn't handle non-finite values.
Results may differ from the reference program's by a relative error of at most 0.025.
Values may be sent and summed in bfloat16 or wider, within the bound.
No kernel may reach another device: no remote copies, remote signals or barrier semaphores. Data moves between devices by JAX's collectives and lax.ppermute only.
A program may use at most 128 MiB of HBM per device.

```python
import math
import jax
import jax.numpy as jnp
import numpy as np
from jax import lax

D = 6144
HEAD_DIM = 128
EXPERT_FF = 4608
TOK_DEV = 64
MOE_TOK = 8
HEAD_COUNT = 64
EXPERTS = 16
FF_DEV = 288
CAP = 2
SEG_LEN = 2048
TOKEN_COUNT = 16384
MOE_TOKENS = 2048
N_SEG = 8
DEVICES = 256


def draw_values(key, part):
    key_sequence = jax.random.split(jax.random.fold_in(key, 11), 3)
    columns = HEAD_COUNT * HEAD_DIM
    column_scale = jnp.exp(jax.random.uniform(key_sequence[0], (1, columns), jnp.float32, math.log(0.3), math.log(3.0)))
    row_scale = jnp.exp(jax.random.uniform(key_sequence[1], (TOKEN_COUNT, 1), jnp.float32, math.log(0.3), math.log(3.0)))
    base = jnp.clip(jax.random.normal(key_sequence[2], (TOKEN_COUNT, columns), jnp.float32), -6.0, 6.0)
    return (base * column_scale * row_scale).astype(jnp.bfloat16)


def draw_log_decay(key, part):
    key_sequence = jax.random.split(jax.random.fold_in(key, 23), 6)
    fast_share = 0.5
    fast_heads = jax.random.uniform(key_sequence[0], (HEAD_COUNT,), jnp.float32) < fast_share
    fast_rate = jnp.exp(jax.random.uniform(key_sequence[1], (HEAD_COUNT,), jnp.float32, math.log(1.0 / 50.0), math.log(1.0 / 30.0)))
    slow_rate = 0.25 / TOKEN_COUNT
    baseline_rate = jnp.where(fast_heads, fast_rate, slow_rate)
    block_count = TOKEN_COUNT // TOK_DEV
    block_multiplier = jnp.exp(jax.random.uniform(key_sequence[2], (block_count, HEAD_COUNT), jnp.float32, math.log(0.5), math.log(2.0)))
    block_multiplier = jnp.repeat(block_multiplier, TOK_DEV, axis=0)
    jaggedness = jax.random.uniform(key_sequence[3], (TOKEN_COUNT, HEAD_COUNT), jnp.float32, 0.5, 1.5)
    spike_locations = jax.random.randint(key_sequence[4], (2, HEAD_COUNT), 0, TOKEN_COUNT)
    token_positions = jnp.arange(TOKEN_COUNT, dtype=jnp.int32)[:, None]
    spike_mask = (token_positions == spike_locations[0][None, :]) | (token_positions == spike_locations[1][None, :])
    spike_magnitude = jax.random.uniform(key_sequence[5], (TOKEN_COUNT, HEAD_COUNT), jnp.float32, 0.22, 0.69)
    decay_rate = baseline_rate[None, :] * block_multiplier * jaggedness + jnp.where(spike_mask, spike_magnitude, 0.0)
    return (-decay_rate).astype(jnp.float32)


def block_scale(key, extent, cuts, smallest, high):
    def one(dim, shards_of):
        draws = jax.random.uniform(jax.random.fold_in(jax.random.fold_in(key, 6), dim), (shards_of,), jnp.float32, smallest / len(cuts), high / len(cuts))
        return jnp.repeat(jnp.exp(draws), extent[dim] // shards_of).reshape((-1,) + (1,) * (len(extent) - dim - 1))

    factor_of = one(*cuts[0])
    for cut in cuts[1:]:
        factor_of = factor_of * one(*cut)
    return factor_of


def deal_out(stream_key, own, number, rows, number_of, top, bound, lean):
    sequence = jax.random.permutation(stream_key, number_of)
    crowded, usual = portions_of(number_of, rows * top, bound, lean, True), portions_of(number_of, rows * top, bound, lean, False)
    places = jnp.arange(number_of)

    def named(lengths, rotation):
        used = int((lengths > 0).sum())
        fixed = max(1, used // 4)
        moved = fixed + (places - fixed + rotation * (used - fixed)) % max(1, number_of - fixed)
        return jnp.zeros((number_of,), jnp.int32).at[sequence[jnp.where(places < fixed, places, moved)]].set(jnp.asarray(lengths, jnp.int32))

    lengths = jnp.where(number % 4 == 0, named(crowded, number // 4), named(usual, number - number // 4 - 1))
    mixed = jax.random.permutation(jax.random.fold_in(own, 3), number_of)
    giver, sink = mixed[0:number_of // 2 * 2:2], mixed[1:number_of // 2 * 2:2]
    margin = jnp.minimum(lengths[giver] - 1, bound - lengths[sink]) // 2
    margin = jnp.where((giver == sequence[0]) | (sink == sequence[0]) | (lengths[sink] == 0), 0, jnp.maximum(margin, 0))
    moved = jax.random.randint(jax.random.fold_in(own, 4), (number_of // 2,), 0, 1 << 20) % (margin + 1)
    lengths = lengths.at[giver].add(-moved).at[sink].add(moved)
    members = jnp.searchsorted(jnp.cumsum(lengths), jnp.arange(rows * top), side="right").astype(jnp.int32)
    table = members.reshape(top, rows).T
    table = table[jax.random.permutation(jax.random.fold_in(own, 1), rows)]
    rotation = jax.random.randint(jax.random.fold_in(own, 2), (rows, 1), 0, top)
    return jnp.take_along_axis(table, (jnp.arange(top)[None, :] + rotation) % top, axis=1)


def portions_of(count, total, limit, slope, full):
    loads = [(1 << 20) // math.isqrt(rank ** slope) + 1 for rank in range(1, count + 1)]
    largest = limit if full else min(limit, max(-(-total // count), total * loads[0] // sum(loads)))
    least = 1 if total - largest >= count - 1 else 0
    counts, rest = [largest] + [least] * (count - 1), total - largest - least * (count - 1)
    while rest > 0:
        free = [i for i in range(1, count) if counts[i] < largest] or [i for i in range(1, count) if counts[i] < limit]
        pool, budget = sum([loads[i] for i in free]), rest
        for i in free:
            addition = min(limit - counts[i], max(1, budget * loads[i] // pool), rest)
            counts[i] = counts[i] + addition
            rest = rest - addition
    return np.array(counts)


def normal_values(own_key, dims, deviation, most, cuts=(), kind=jnp.bfloat16):
    values = jax.random.normal(own_key, dims, jnp.float32) * deviation
    if len(cuts) > 0:
        values = block_scale(own_key, dims, cuts, -0.22, 0.18) * values
    return jnp.clip(values, min=-most, max=most).astype(kind)


def setup_inputs(seed: int = 0) -> dict:
    arg_keys = jax.random.split(jax.random.key(seed), 11)
    queries = normal_values(arg_keys[0], (TOKEN_COUNT, HEAD_COUNT * HEAD_DIM), 1.0, 6.0, ((0, 256),))
    keys = normal_values(arg_keys[1], (TOKEN_COUNT, HEAD_COUNT * HEAD_DIM), (HEAD_DIM ** -0.5), 1.25, ((0, 256),))
    values = draw_values(jax.random.fold_in(arg_keys[10], 71), 0)
    log_decay = draw_log_decay(jax.random.fold_in(arg_keys[10], 71), 0)
    out_gain = jnp.clip(1.0 + 0.18 * jax.random.normal(arg_keys[4], (HEAD_COUNT * HEAD_DIM,), jnp.float32), 0.1, 1.9)
    out_proj = normal_values(arg_keys[5], (HEAD_COUNT * HEAD_DIM, D), (HEAD_COUNT * HEAD_DIM) ** -0.5, 0.0625, ((0, 32), (1, 8)))
    experts_keys = jax.random.split(jax.random.fold_in(arg_keys[6], 1), MOE_TOKENS // MOE_TOK)
    experts_turns = jax.random.permutation(jax.random.fold_in(arg_keys[6], 3), MOE_TOKENS // MOE_TOK)
    experts = jax.vmap(lambda own, number: deal_out(jax.random.fold_in(arg_keys[6], 2), own, number, MOE_TOK, EXPERTS, 2, CAP, 2))(experts_keys, experts_turns).reshape((MOE_TOKENS, 2))
    gates = jnp.clip(0.2 + 0.8 * jax.random.uniform(arg_keys[7], (MOE_TOKENS, 2), jnp.float32) ** block_scale(arg_keys[7], (MOE_TOKENS, 2), ((0, 256),), -0.2, 0.2), 0.2, 1.0)
    up_weight = normal_values(arg_keys[8], (2 * EXPERTS, D, EXPERT_FF // 2), D ** -0.5, 0.078125, ((0, 32), (2, 8)))
    down_weight = normal_values(arg_keys[9], (2 * EXPERTS, EXPERT_FF // 2, D), EXPERT_FF ** -0.5, 0.09375, ((0, 32), (1, 8)))
    return {"queries": queries, "keys": keys, "values": values, "log_decay": log_decay, "out_gain": out_gain, "out_proj": out_proj, "experts": experts, "gates": gates, "up_weight": up_weight, "down_weight": down_weight}


def reference(queries, keys, values, log_decay, out_gain, out_proj, experts, gates, up_weight, down_weight):
    highest = lax.Precision.HIGHEST
    grid = (N_SEG, SEG_LEN, HEAD_COUNT, HEAD_DIM)
    query_groups = queries.reshape(grid).astype(jnp.float32)
    key_groups = keys.reshape(grid).astype(jnp.float32)
    value_groups = values.reshape(grid).astype(jnp.float32)
    decay_groups = log_decay.reshape(N_SEG, SEG_LEN, HEAD_COUNT)
    causal_mask = jnp.arange(SEG_LEN)[:, None] >= jnp.arange(SEG_LEN)[None, :]

    def head_inside(inputs):
        query_head, key_head, value_head, cum_head = inputs
        log_gap = cum_head[:, None] - cum_head[None, :]
        weight = jnp.where(causal_mask, jnp.exp(jnp.where(causal_mask, log_gap, 0.0)), 0.0)
        scores = jnp.dot(query_head, key_head.T, precision=highest)
        mixing = lax.optimization_barrier((scores * weight).astype(jnp.bfloat16)).astype(jnp.float32)
        return jnp.dot(mixing, value_head, precision=highest)

    def group_step(state, inputs):
        query_block, key_block, value_block, decay_block = inputs
        cumulative = jnp.cumsum(decay_block, axis=0)
        inside = lax.map(head_inside, (query_block.transpose(1, 0, 2), key_block.transpose(1, 0, 2), value_block.transpose(1, 0, 2), cumulative.T)).transpose(1, 0, 2)
        outside = jnp.exp(cumulative)[:, :, None] * jnp.einsum('thd,hde->the', query_block, state, precision=highest)
        mixture = (inside + outside).astype(jnp.bfloat16)
        ending = cumulative[-1]
        to_end = jnp.exp(ending[None, :] - cumulative)
        local_state = jnp.einsum('sh,shd,she->hde', to_end, key_block, value_block, precision=highest)
        new_state = jnp.exp(ending)[:, None, None] * state + local_state
        return (new_state, mixture)
    start_state = jnp.zeros((HEAD_COUNT, HEAD_DIM, HEAD_DIM), jnp.float32)
    final_state, mixtures = lax.scan(group_step, start_state, (query_groups, key_groups, value_groups, decay_groups))
    heads_mix = mixtures.reshape(TOKEN_COUNT, HEAD_COUNT * HEAD_DIM).astype(jnp.float32)
    inv_rms = lax.rsqrt(lax.optimization_barrier(jnp.mean(heads_mix * heads_mix, axis=1, keepdims=True)) + 1e-06)
    attn_out = (heads_mix * inv_rms * out_gain[None, :]).astype(jnp.bfloat16)
    selected = attn_out.reshape(MOE_TOKENS, TOKEN_COUNT // MOE_TOKENS, HEAD_COUNT * HEAD_DIM)[:, 0]
    moe_in = jnp.dot(selected, out_proj, preferred_element_type=jnp.float32).astype(jnp.bfloat16)
    flattened = experts.reshape(DEVICES, 2 * MOE_TOK)
    onehot = (flattened[:, :, None] == jnp.arange(EXPERTS, dtype=jnp.int32)[None, None, :]).astype(jnp.int32)
    earlier = jnp.cumsum(onehot, axis=1) - onehot
    position = lax.optimization_barrier(jnp.sum(earlier * onehot, axis=2)).astype(jnp.int32)
    slot_of = position.reshape(DEVICES, MOE_TOK, 2)
    expert_of = experts.reshape(DEVICES, MOE_TOK, 2)
    rows_by_device = moe_in.reshape(DEVICES, MOE_TOK, D).astype(jnp.float32)
    capacity_ids = jnp.arange(CAP, dtype=jnp.int32)

    def per_expert(expert):
        matches = (expert_of == expert)[:, :, :, None] & (slot_of[:, :, :, None] == capacity_ids[None, None, None, :])
        chosen = jnp.any(matches, axis=2).astype(jnp.float32)
        row_data = jnp.einsum('dtc,dtk->dck', chosen, rows_by_device, precision=highest)
        row_data = row_data.astype(jnp.bfloat16).reshape(DEVICES * CAP, D)
        running = jnp.zeros((DEVICES * CAP, D), jnp.float32)
        for half_index in range(2):
            row_index = (2 * expert + half_index).astype(jnp.int32)
            up_half = lax.dynamic_index_in_dim(up_weight, row_index, 0, keepdims=False)
            down_half = lax.dynamic_index_in_dim(down_weight, row_index, 0, keepdims=False)
            hidden = jax.nn.silu(jnp.dot(row_data, up_half, preferred_element_type=jnp.float32)).astype(jnp.bfloat16)
            hidden_pieces = hidden.reshape(DEVICES * CAP, N_SEG, FF_DEV).astype(jnp.float32)
            down_pieces = down_half.reshape(N_SEG, FF_DEV, D).astype(jnp.float32)
            slice_terms = jnp.einsum('rgk,gkd->grd', hidden_pieces, down_pieces, precision=highest)
            rounded = lax.optimization_barrier(slice_terms.astype(jnp.bfloat16)).astype(jnp.float32)
            running = running + lax.optimization_barrier(jnp.sum(rounded, axis=0))
        return running
    results = lax.map(per_expert, jnp.arange(EXPERTS, dtype=jnp.int32))
    device_index = jnp.arange(DEVICES, dtype=jnp.int32)[:, None, None]
    flat_index = (expert_of * (DEVICES * CAP) + device_index * CAP + slot_of).astype(jnp.int32)
    picked = results.reshape(EXPERTS * DEVICES * CAP, D)[flat_index.reshape(-1)].reshape(DEVICES, MOE_TOK, 2, D)
    weighted = lax.optimization_barrier(jnp.sum(picked * gates.reshape(DEVICES, MOE_TOK, 2, 1), axis=2))
    moe_out = weighted.astype(jnp.bfloat16).reshape(MOE_TOKENS, D)
    return (attn_out, moe_out)
```

```python
import jax
import jax.numpy as jnp
from jax import lax
from jax.experimental import pallas as pl
from jax.experimental.pallas import tpu as pltpu
from jax.sharding import Mesh
from jax.sharding import PartitionSpec as P

SEG = ("y", "c")
EP = ("z", "x")
SEG_EP = SEG + EP

HEAD = 128
PAIR = 2 * HEAD
EPS = 1e-06
bf16 = jnp.bfloat16
f32 = jnp.float32


def shifted(v, axis, by):
    n = lax.axis_size(axis)
    return lax.ppermute(v, axis, [(i, (i + by) % n) for i in range(n)])


def kernel_call(body, outs, args, scalars=0, flops=0, steps=None, blocks=None):
    moved = sum(a.size * a.dtype.itemsize for a in list(args) + list(outs))
    tables = [pl.BlockSpec(memory_space=pltpu.SMEM) for _ in range(scalars)]
    arrays = list(args[scalars:]) + list(outs)
    if steps is None:
        specs = [pl.BlockSpec(memory_space=pltpu.VMEM) for _ in arrays]
    else:
        specs = []
        for a, dim in zip(arrays, blocks):
            shape = tuple(n // steps if i == dim else n for i, n in enumerate(a.shape))
            index = lambda i, dim=dim, rank=len(shape): tuple(i if j == dim else 0 for j in range(rank))
            specs.append(pl.BlockSpec(shape, index))
    inputs = len(args) - scalars
    if steps is not None:
        args = [
            pltpu.with_memory_space_constraint(a, pltpu.HBM)
            if i >= scalars and a.size * a.dtype.itemsize >= 1 << 18
            else a
            for i, a in enumerate(args)
        ]
    return pl.pallas_call(
        body,
        out_shape=tuple(outs),
        grid=() if steps is None else (steps,),
        in_specs=tables + specs[:inputs],
        out_specs=tuple(specs[inputs:]),
        compiler_params=pltpu.CompilerParams(vmem_limit_bytes=2 * moved + (8 << 20)),
        cost_estimate=pl.CostEstimate(flops=flops, transcendentals=0, bytes_accessed=moved),
    )(*args)


def struct(shape, dtype):
    return jax.ShapeDtypeStruct(shape, dtype)


def dot(a, b, dims):
    return lax.dot_general(a, b, (dims, ((), ())), preferred_element_type=f32)


def pack_pair_body(ids, k, v, *outs):
    groups = k.shape[1] // (4 * PAIR)
    for d in range(4):
        at = lax.rem(ids[0] + d, 4) * PAIR
        for g in range(groups):
            cols = pl.ds(pl.multiple_of(at + g * 4 * PAIR, PAIR), PAIR)
            outs[d][0, :, g * PAIR : (g + 1) * PAIR] = k[:, cols]
            outs[d][1, :, g * PAIR : (g + 1) * PAIR] = v[:, cols]


def pack_body(ids, q, *outs):
    groups = q.shape[1] // (4 * PAIR)
    for d in range(4):
        at = lax.rem(ids[0] + d, 4) * PAIR
        for g in range(groups):
            cols = pl.ds(pl.multiple_of(at + g * 4 * PAIR, PAIR), PAIR)
            outs[d][:, g * PAIR : (g + 1) * PAIR] = q[:, cols]


def queries_of(pieces, h):
    return jnp.concatenate([p[:, h * HEAD : (h + 1) * HEAD] for p in pieces], axis=0)


def rows_of(pieces, lead, h):
    cols = slice(h * HEAD, (h + 1) * HEAD)
    return jnp.concatenate([p[lead, :, cols] for p in pieces], axis=0)


def chunk_state_body(kv0, kv1, kv2, kv3, rel_col, tot_row, out):
    pieces = (kv0, kv1, kv2, kv3)
    to_end = jnp.exp(tot_row[0] - rel_col[0])
    for h in range(rel_col.shape[2]):
        k = rows_of(pieces, 0, h).astype(f32)
        weighted = (k * to_end[:, h : h + 1]).astype(bf16)
        state = dot(weighted, rows_of(pieces, 1, h), ((0,), (0,)))
        out[h // 2, (h % 2) * HEAD : (h % 2 + 1) * HEAD, :] = state.astype(bf16)


def inside_body(ids, q0, q1, q2, q3, kv0, kv1, kv2, kv3, rel_col, rel_row, out):
    qs, kvs = (q0, q1, q2, q3), (kv0, kv1, kv2, kv3)
    length, block = rel_col.shape[1], q0.shape[0]

    def positions(axis):
        i = lax.broadcasted_iota(jnp.int32, (length, length), axis)
        return ((ids[0] + 4 - i // block) & 3) * block + (i & (block - 1))

    causal = positions(0) >= positions(1)
    for h in range(rel_col.shape[2]):
        gap = rel_col[0, :, h : h + 1] - rel_row[0, h : h + 1, :]
        weight = jnp.exp(jnp.where(causal, gap, -jnp.inf))
        scores = dot(queries_of(qs, h), rows_of(kvs, 0, h), ((1,), (1,)))
        mixing = (scores * weight).astype(bf16)
        out[:, h * HEAD : (h + 1) * HEAD] = dot(mixing, rows_of(kvs, 1, h), ((1,), (0,)))


def group_state_body(dec, s, info, out):
    for h in range(2):
        rows = slice(h * HEAD, (h + 1) * HEAD)
        total = s[0, rows, :].astype(f32)
        for z in range(1, s.shape[0]):
            total = total * dec[h, z] + s[z, rows, :].astype(f32)
        out[rows, :] = total.astype(bf16)
    out[PAIR:, :] = info[...]


def prefix_body(ids, dec, s, g0, g1, out):
    own = ids[1] * 2 + ids[2]
    each = g0.shape[0] // 4
    slots = [(g, d * each, r) for r, g in enumerate((g0, g1)) for d in range(4)]
    group = [
        lax.rem(ids[1] + 4 - d, 4) * 2 + ((ids[2] + r) & 1) for r in range(2) for d in range(4)
    ]
    for h in range(2):
        rows = slice(h * HEAD, (h + 1) * HEAD)

        def ending(slot):
            g, at, _ = slots[slot]
            first = at + PAIR + 8 + 3 * h
            e = [g[first + k : first + k + 1, :].astype(f32) for k in range(3)]
            return (e[0] + e[1]) + e[2]

        ends = [ending(slot) for slot in range(8)]
        state = jnp.zeros((HEAD, HEAD), f32)
        for i, (g, at, _) in enumerate(slots):
            gap = jnp.zeros((1, HEAD), f32)
            for j in range(8):
                between = (group[i] < group[j]) & (group[j] < own)
                gap = gap + jnp.where(between, 1.0, 0.0) * ends[j]
            factor = jnp.where(group[i] < own, 1.0, 0.0) * jnp.exp(gap)
            state = state + factor * g[at + h * HEAD : at + (h + 1) * HEAD, :].astype(f32)
        for z in range(s.shape[0]):
            out[z, rows, :] = state.astype(bf16)
            state = state * dec[h, z] + s[z, rows, :].astype(f32)


def mix_body(inside, q0, q1, q2, q3, prefix, rel_col, gain, m0, m1, m2, m3, rows_out, squares):
    qs, outs = (q0, q1, q2, q3), (m0, m1, m2, m3)
    length, block = rel_col.shape[1], q0.shape[0]
    picked = length // 8
    step, steps = pl.program_id(0), pl.num_programs(0)
    width = inside.shape[1]
    from_start = jnp.exp(rel_col[0])
    row = lax.broadcasted_iota(jnp.int32, (picked, length), 0)
    col = lax.broadcasted_iota(jnp.int32, (picked, length), 1)
    pick = (col == row * 8).astype(f32).astype(bf16)

    @pl.when(step == 0)
    def _():
        squares[...] = jnp.zeros_like(squares)

    for h in range(rel_col.shape[2]):
        cols = slice(h * HEAD, (h + 1) * HEAD)
        outside = dot(
            queries_of(qs, h),
            prefix[h // 2, (h % 2) * HEAD : (h % 2 + 1) * HEAD, :],
            ((1,), (0,)),
        )
        mixed = (inside[:, cols] + from_start[:, h : h + 1] * outside).astype(bf16)
        for d in range(4):
            outs[d][:, cols] = mixed[d * block : (d + 1) * block]
        rows = dot(pick, mixed, ((1,), (0,)))
        squares[...] += rows * rows
        at = pl.multiple_of(step * width + h * HEAD, HEAD)
        rows_out[:, pl.ds(at, HEAD)] = (rows * gain[:, cols]).astype(bf16)

    @pl.when(step == steps - 1)
    def _():
        total = jnp.sum(squares[...], axis=1, keepdims=True)
        high = total.astype(bf16).astype(f32)
        lane = lax.broadcasted_iota(jnp.int32, (picked, HEAD), 1)
        extra = jnp.where(lane == 0, high, jnp.where(lane == 1, total - high, 0.0))
        rows_out[:, rows_out.shape[1] - HEAD :] = extra.astype(bf16)


def project_body(r0, r1, weight, p0, p1, p2, p3):
    outs = (p0, p1, p2, p3)
    features, width = weight.shape
    for half, r in enumerate((r0, r1)):
        terms = dot(r[:, :features], weight[...], ((1,), (0,)))
        terms = terms.reshape(4, 4, 8, width)
        extra = r[:, features:].astype(f32).reshape(4, 4, 8, HEAD)
        for d in range(4):
            at = slice(half * 32, (half + 1) * 32)
            outs[d][at, :width] = terms[:, d].reshape(32, width).astype(bf16)
            outs[d][at, width:] = extra[:, d].reshape(32, HEAD).astype(bf16)


def dispatch_body(p0, p1, p2, p3, slots, out, *, features):
    width = out.shape[2]
    total = (p0[...].astype(f32) + p1[...].astype(f32)) + (p2[...].astype(f32) + p3[...].astype(f32))
    squares = total[:, width : width + 1] + total[:, width + 1 : width + 2]
    scale = lax.rsqrt(squares * (1.0 / features) + EPS)
    moe_in = (total[:, :width] * scale).astype(bf16)
    per = out.shape[1]
    count = (out.shape[0] // 2) * per
    target = lax.broadcasted_iota(jnp.int32, (count, total.shape[0]), 0)
    chosen = (target == slots[0:1, :]) | (target == slots[1:2, :])
    sent = dot(chosen.astype(f32).astype(bf16), moe_in, ((1,), (0,))).astype(bf16)
    for e in range(out.shape[0] // 2):
        block = sent[e * per : (e + 1) * per]
        out[2 * e] = block
        out[2 * e + 1] = block


def up_body(ids, own, other, w0, w1, w2, w3, *outs):
    width = own.shape[1]
    mine = pl.ds(pl.multiple_of(ids[2] * width, HEAD), width)
    rest = pl.ds(pl.multiple_of((1 - ids[2]) * width, HEAD), width)
    for w, out in zip((w0, w1, w2, w3), outs):
        part = dot(w[:, mine], own[...], ((1,), (1,)))
        part = part + dot(w[:, rest], other[...], ((1,), (1,)))
        out[...] = part.astype(bf16)


def down_body(ids, h0, h1, h2, h3, w0, w1, w2, w3, keep, send):
    width = keep.shape[1]
    mine = pl.ds(pl.multiple_of(ids[2] * width, HEAD), width)
    rest = pl.ds(pl.multiple_of((1 - ids[2]) * width, HEAD), width)
    hs, ws = (h0, h1, h2, h3), (w0, w1, w2, w3)
    send[...] = sum(dot(h[...], w[:, rest], ((0,), (0,))) for h, w in zip(hs, ws)).astype(bf16)
    keep[...] = sum(dot(h[...], w[:, mine], ((0,), (0,))) for h, w in zip(hs, ws))


def combine_body(ids, back, table, out):
    count = back.shape[0]
    lane = lax.broadcasted_iota(jnp.int32, (table.shape[0], count), 1)
    slot = ((lane >> 5) * 16 + (lane & 15)).astype(f32)
    gate = jnp.where(slot == table[:, 0:1], table[:, 2:3], 0.0) + jnp.where(
        slot == table[:, 1:2], table[:, 3:4], 0.0
    )
    high = gate.astype(bf16)
    low = (gate - high.astype(f32)).astype(bf16)
    total = dot(high, back[...], ((1,), (0,))) + dot(low, back[...], ((1,), (0,)))
    for r in range(2):
        for d in range(4):
            seg = lax.rem(ids[1] + 4 - d, 4) * 2 + ((ids[2] + r) & 1)
            at = (r * 4 + d) * 8
            out[seg] = total[at : at + 8].astype(bf16)


def norm_body(ids, m0, m1, m2, m3, gain, out):
    pieces = (m0, m1, m2, m3)
    width = m0.shape[1]
    total = jnp.zeros((m0.shape[0], 1), f32)
    for m in pieces:
        as_float = m[...].astype(f32)
        total = total + jnp.sum(as_float * as_float, axis=1, keepdims=True)
    scale = lax.rsqrt(total * (1.0 / (4 * width)) + EPS)
    for d, m in enumerate(pieces):
        at = lax.rem(ids[0] + d, 4) * PAIR
        for g in range(width // PAIR):
            cols = pl.ds(pl.multiple_of(at + g * 4 * PAIR, PAIR), PAIR)
            values = m[:, g * PAIR : (g + 1) * PAIR].astype(f32)
            out[:, cols] = (values * scale * gain[:, cols]).astype(bf16)


def over_seg(v):
    mine = jnp.concatenate([v] + [shifted(v, "y", d) for d in range(1, 4)], axis=0)
    return mine, shifted(mine, "c", 1)


def in_three(v):
    high = lax.reduce_precision(v, 8, 7)
    middle = lax.reduce_precision(v - high, 8, 7)
    return high, middle, lax.reduce_precision(v - high - middle, 8, 7)


def slot_ids(experts, expert_count):
    flat = experts.reshape(-1)
    onehot = (flat[:, None] == jnp.arange(expert_count, dtype=jnp.int32)[None, :]).astype(jnp.int32)
    earlier = flat[:, None] == flat[None, :]
    before = jnp.arange(flat.size)[:, None] > jnp.arange(flat.size)[None, :]
    position = jnp.sum((earlier & before).astype(jnp.int32), axis=1)
    return flat.reshape(experts.shape), position.reshape(experts.shape)


def on_device(
    queries, keys, values, log_decay, out_gain, out_proj, experts, gates, up_weight, down_weight
):
    x, y, c = lax.axis_index("x"), lax.axis_index("y"), lax.axis_index("c")
    ids = jnp.stack([x, y, c]).astype(jnp.int32)
    tokens, all_features = queries.shape
    features = all_features // 4
    heads = features // HEAD
    length = 4 * tokens
    n_z = lax.axis_size("z")
    model_slice = out_proj.shape[1]
    rows_dev = experts.shape[0]
    expert_count = 4 * n_z // 2

    kv_out = kernel_call(
        pack_pair_body, [struct((2, tokens, features), bf16)] * 4, (ids, keys, values), scalars=1
    )
    kv_out = list(kv_out)
    kv = [None] + [shifted(kv_out[d], "x", d) for d in range(1, 4)]
    queries, kv[1] = lax.optimization_barrier((queries, kv[1]))
    q_out = kernel_call(pack_body, [struct((tokens, features), bf16)] * 4, (ids, queries), scalars=1)
    q = [q_out[0]] + [shifted(q_out[d], "x", d) for d in range(1, 4)]

    weight_out = lax.all_gather(out_proj, "z", axis=0, tiled=True)

    def sliced(w):
        quarter = w.shape[1] // 4
        return [
            lax.dynamic_slice_in_dim(w, ((y + d) % 4) * quarter, quarter, 1) for d in range(4)
        ]

    def over_y(pieces):
        return [pieces[0]] + [shifted(pieces[d], "y", d) for d in range(1, 4)]

    up = sliced(up_weight[0].T)
    kv[0], log_decay, *up = lax.optimization_barrier((kv_out[0], log_decay, *up))
    up = over_y(up)

    decay = log_decay.T.reshape(2 * n_z, length)
    upto = (
        jnp.arange(length, dtype=jnp.int32)[:, None] <= jnp.arange(length, dtype=jnp.int32)[None, :]
    ).astype(f32)
    rel_own = jnp.dot(decay, upto, precision=lax.Precision.HIGHEST).reshape(2, n_z, length)
    chunk_total = rel_own[:, :, -1]
    chunk_decay = jnp.exp(chunk_total)
    rel = lax.all_to_all(rel_own.transpose(1, 0, 2), "z", 0, 0, tiled=True).reshape(heads, length)
    by_source = rel.reshape(heads, 4, tokens)
    order = (x + 4 - jnp.arange(4, dtype=jnp.int32)) % 4
    rel_row = jnp.concatenate(
        [lax.dynamic_index_in_dim(by_source, order[d], 1, keepdims=False) for d in range(4)], axis=1
    )
    steps = 4
    rel_row = rel_row.reshape(steps, heads // steps, length)
    rel_col = rel_row.transpose(0, 2, 1)
    tot_row = rel[:, -1].reshape(steps, 1, heads // steps)

    expert, position = slot_ids(experts, expert_count)
    group_total = jnp.repeat(jnp.stack(in_three(jnp.sum(chunk_total, axis=1)), 1).reshape(6, 1), 128, 1)
    columns = [expert.astype(f32), position.astype(f32), *in_three(gates)]
    info = jnp.concatenate(columns + [jnp.zeros((rows_dev, 128 - 2 * len(columns)), f32)], axis=1)
    info = jnp.concatenate([info, group_total, jnp.zeros((2, 128), f32)], axis=0).astype(bf16)

    states = kernel_call(
        chunk_state_body,
        [struct((n_z, PAIR, HEAD), bf16)],
        (*kv, rel_col, tot_row),
        flops=2 * length * features * HEAD,
        steps=steps,
        blocks=(2, 2, 2, 2, 0, 0, 0),
    )[0]
    states, weight_out, *down = lax.optimization_barrier(
        (states, weight_out, *sliced(down_weight[0]))
    )
    down = over_y(down)
    states = lax.all_to_all(states, "z", 0, 0, tiled=True)
    inside = kernel_call(
        inside_body,
        [struct((length, features), f32)],
        (ids, *q, *kv, rel_col, rel_row),
        scalars=1,
        flops=4 * length * length * features,
        steps=steps,
        blocks=(1,) * 4 + (2,) * 4 + (0, 0, 1),
    )[0]
    states, *up = lax.optimization_barrier((states, *up))
    local = kernel_call(
        group_state_body, [struct((PAIR + 16, HEAD), bf16)], (chunk_decay, states, info), scalars=1
    )[0]
    *groups, down[2] = lax.optimization_barrier((*over_seg(local), down[2]))
    prefix = kernel_call(
        prefix_body,
        [struct((n_z, PAIR, HEAD), bf16)],
        (ids, chunk_decay, states, *groups),
        scalars=2,
    )[0]
    prefix = lax.all_to_all(prefix, "z", 0, 0, tiled=True)
    info = jnp.concatenate(
        [g.reshape(4, PAIR + 16, HEAD)[:, PAIR : PAIR + rows_dev] for g in groups], axis=0
    ).astype(f32)
    slot = jnp.arange(8, dtype=jnp.int32)
    group = ((y + 4 - slot % 4) % 4) * 2 + (c + slot // 4) % 2
    slots = info[..., 0:2] * 16.0 + group[:, None, None].astype(f32) * 2.0 + info[..., 2:4]
    slots = slots.reshape(8 * rows_dev, 2)
    gate = (info[..., 4:6] + info[..., 6:8] + info[..., 8:10]).reshape(8 * rows_dev, 2)
    slot_rows = slots.T.astype(jnp.int32)
    combine_table = jnp.concatenate([slots, gate, jnp.zeros((8 * rows_dev, 124), f32)], axis=1)
    gain_own = lax.dynamic_index_in_dim(
        out_gain.reshape(n_z, 4, PAIR), x, 1, keepdims=False
    ).reshape(1, features)
    *mixed, rows, _ = kernel_call(
        mix_body,
        [struct((tokens, features), bf16)] * 4
        + [struct((length // 8, features + HEAD), bf16), struct((length // 8, HEAD), f32)],
        (inside, *q, prefix, rel_col, gain_own),
        flops=2 * length * features * HEAD,
        steps=steps,
        blocks=(1,) * 5 + (0, 0, 1) + (1,) * 4 + (None, None),
    )

    terms = kernel_call(
        project_body,
        [struct((8 * rows_dev, model_slice + HEAD), bf16)] * 4,
        (*over_seg(rows), weight_out),
        flops=2 * length * features * model_slice,
    )
    terms = [terms[0]] + [shifted(terms[d], "x", -d) for d in range(1, 4)]
    outgoing = kernel_call(
        lambda *refs: dispatch_body(*refs, features=all_features),
        [struct((2 * expert_count, 16, model_slice), bf16)],
        (*terms, slot_rows),
    )[0]
    arrived = lax.all_to_all(outgoing, EP, 0, 0, tiled=True).reshape(-1, model_slice)
    arrived, down[1], down[3], combine_table = lax.optimization_barrier(
        (arrived, down[1], down[3], combine_table)
    )

    hidden_dev = up[0].shape[0]
    parts = kernel_call(
        up_body,
        [struct((hidden_dev, arrived.shape[0]), bf16)] * 4,
        (ids, arrived, shifted(arrived, "c", 1), *up),
        scalars=1,
        flops=16 * arrived.size * hidden_dev,
    )
    parts = [parts[0]] + [shifted(parts[d], "y", -d) for d in range(1, 4)]
    hidden = jax.nn.silu(sum(p.astype(f32) for p in parts)).astype(bf16)
    mixed = [mixed[0]] + [shifted(mixed[d], "x", -d) for d in range(1, 4)]
    hiddens = [hidden] + [shifted(hidden, "y", d) for d in range(1, 4)]
    keep, send = kernel_call(
        down_body,
        [struct(arrived.shape, f32), struct(arrived.shape, bf16)],
        (ids, *hiddens, *down),
        scalars=1,
        flops=16 * arrived.size * hidden_dev,
    )
    result = (keep + shifted(send, "c", 1).astype(f32)).astype(bf16)
    back = lax.all_to_all(
        result.reshape(outgoing.shape), EP, 0, 0, tiled=True
    ).reshape(-1, model_slice)
    mine = kernel_call(
        combine_body,
        [struct((8, rows_dev, model_slice), bf16)],
        (ids, back, combine_table),
        scalars=1,
    )[0]
    moe_out = lax.all_to_all(mine, SEG, 0, 0, tiled=True).transpose(1, 0, 2).reshape(rows_dev, -1)

    attn_out = kernel_call(
        norm_body,
        [struct((tokens, all_features), bf16)],
        (ids, *mixed, out_gain.reshape(1, -1)),
        scalars=1,
    )[0]
    return attn_out, moe_out


def solution(mesh):
    torus = Mesh(mesh.devices.reshape(4, 2, 8, 4), SEG_EP)
    placed = (
        P(SEG_EP, None),
        P(SEG_EP, None),
        P(SEG_EP, None),
        P(SEG, EP),
        P(),
        P(EP, SEG),
        P(SEG_EP, None),
        P(SEG_EP, None),
        P(EP, None, SEG),
        P(EP, SEG, None),
    )
    return jax.shard_map(
        on_device,
        mesh=torus,
        in_specs=placed,
        out_specs=(P(SEG_EP, None), P(SEG_EP, None)),
        check_vma=False,
    )
```

```python
import jax
import jax.numpy as jnp
from jax import lax
from jax.experimental import pallas as pl
from jax.experimental.pallas import tpu as pltpu
from jax.sharding import Mesh
from jax.sharding import PartitionSpec as P

SEG = ("y", "c")
EP = ("z", "x")
SEG_EP = SEG + EP

HEAD = 128
PAIR = 2 * HEAD
EPS = 1e-06
bf16 = jnp.bfloat16
f32 = jnp.float32


def shifted(v, axis, by):
    n = lax.axis_size(axis)
    return lax.ppermute(v, axis, [(i, (i + by) % n) for i in range(n)])


def kernel_call(body, outs, args, scalars=0, flops=0, steps=None, blocks=None):
    moved = sum(a.size * a.dtype.itemsize for a in list(args) + list(outs))
    tables = [pl.BlockSpec(memory_space=pltpu.SMEM) for _ in range(scalars)]
    arrays = list(args[scalars:]) + list(outs)
    if steps is None:
        specs = [pl.BlockSpec(memory_space=pltpu.VMEM) for _ in arrays]
    else:
        specs = []
        for a, dim in zip(arrays, blocks):
            shape = tuple(n // steps if i == dim else n for i, n in enumerate(a.shape))
            index = lambda i, dim=dim, rank=len(shape): tuple(i if j == dim else 0 for j in range(rank))
            specs.append(pl.BlockSpec(shape, index))
    inputs = len(args) - scalars
    if steps is not None:
        args = [
            pltpu.with_memory_space_constraint(a, pltpu.HBM)
            if i >= scalars and a.dtype == bf16 and a.size >= 1 << 17
            else a
            for i, a in enumerate(args)
        ]
    return pl.pallas_call(
        body,
        out_shape=tuple(outs),
        grid=() if steps is None else (steps,),
        in_specs=tables + specs[:inputs],
        out_specs=tuple(specs[inputs:]),
        compiler_params=pltpu.CompilerParams(vmem_limit_bytes=2 * moved + (8 << 20)),
        cost_estimate=pl.CostEstimate(flops=flops, transcendentals=0, bytes_accessed=moved),
    )(*args)


def struct(shape, dtype):
    return jax.ShapeDtypeStruct(shape, dtype)


def dot(a, b, dims):
    return lax.dot_general(a, b, (dims, ((), ())), preferred_element_type=f32)


def pack_pair_body(ids, k, v, *outs):
    groups = k.shape[1] // (4 * PAIR)
    for d in range(4):
        at = lax.rem(ids[0] + d, 4) * PAIR
        for g in range(groups):
            cols = pl.ds(pl.multiple_of(at + g * 4 * PAIR, PAIR), PAIR)
            outs[d][0, :, g * PAIR : (g + 1) * PAIR] = k[:, cols]
            outs[d][1, :, g * PAIR : (g + 1) * PAIR] = v[:, cols]


def pack_body(ids, q, *outs):
    groups = q.shape[1] // (4 * PAIR)
    for d in range(4):
        at = lax.rem(ids[0] + d, 4) * PAIR
        for g in range(groups):
            cols = pl.ds(pl.multiple_of(at + g * 4 * PAIR, PAIR), PAIR)
            outs[d][:, g * PAIR : (g + 1) * PAIR] = q[:, cols]


def queries_of(pieces, h):
    return jnp.concatenate([p[:, h * HEAD : (h + 1) * HEAD] for p in pieces], axis=0)


def rows_of(pieces, lead, h):
    cols = slice(h * HEAD, (h + 1) * HEAD)
    return jnp.concatenate([p[lead, :, cols] for p in pieces], axis=0)


def chunk_state_body(kv0, kv1, kv2, kv3, rel_col, tot_row, out):
    pieces = (kv0, kv1, kv2, kv3)
    to_end = jnp.exp(tot_row[0] - rel_col[0])
    for h in range(rel_col.shape[2]):
        k = rows_of(pieces, 0, h).astype(f32)
        weighted = (k * to_end[:, h : h + 1]).astype(bf16)
        state = dot(weighted, rows_of(pieces, 1, h), ((0,), (0,)))
        out[h // 2, (h % 2) * HEAD : (h % 2 + 1) * HEAD, :] = state.astype(bf16)


def inside_body(ids, q0, q1, q2, q3, kv0, kv1, kv2, kv3, rel_col, rel_row, out):
    qs, kvs = (q0, q1, q2, q3), (kv0, kv1, kv2, kv3)
    length, block = rel_col.shape[1], q0.shape[0]

    def positions(axis):
        i = lax.broadcasted_iota(jnp.int32, (length, length), axis)
        return ((ids[0] + 4 - i // block) & 3) * block + (i & (block - 1))

    causal = positions(0) >= positions(1)
    for h in range(rel_col.shape[2]):
        gap = rel_col[0, :, h : h + 1] - rel_row[0, h : h + 1, :]
        weight = jnp.exp(jnp.where(causal, gap, -jnp.inf))
        scores = dot(queries_of(qs, h), rows_of(kvs, 0, h), ((1,), (1,)))
        mixing = (scores * weight).astype(bf16)
        out[:, h * HEAD : (h + 1) * HEAD] = dot(mixing, rows_of(kvs, 1, h), ((1,), (0,)))


def group_state_body(dec, s, info, out):
    for h in range(2):
        rows = slice(h * HEAD, (h + 1) * HEAD)
        total = s[0, rows, :].astype(f32)
        for z in range(1, s.shape[0]):
            total = total * dec[h, z] + s[z, rows, :].astype(f32)
        out[rows, :] = total.astype(bf16)
    out[PAIR:, :] = info[...]


def prefix_body(ids, dec, s, g0, g1, out):
    own = ids[1] * 2 + ids[2]
    each = g0.shape[0] // 4
    slots = [(g, d * each, r) for r, g in enumerate((g0, g1)) for d in range(4)]
    group = [
        lax.rem(ids[1] + 4 - d, 4) * 2 + ((ids[2] + r) & 1) for r in range(2) for d in range(4)
    ]
    for h in range(2):
        rows = slice(h * HEAD, (h + 1) * HEAD)

        def ending(slot):
            g, at, _ = slots[slot]
            first = at + PAIR + 8 + 3 * h
            e = [g[first + k : first + k + 1, :].astype(f32) for k in range(3)]
            return (e[0] + e[1]) + e[2]

        ends = [ending(slot) for slot in range(8)]
        state = jnp.zeros((HEAD, HEAD), f32)
        for i, (g, at, _) in enumerate(slots):
            gap = jnp.zeros((1, HEAD), f32)
            for j in range(8):
                between = (group[i] < group[j]) & (group[j] < own)
                gap = gap + jnp.where(between, 1.0, 0.0) * ends[j]
            factor = jnp.where(group[i] < own, 1.0, 0.0) * jnp.exp(gap)
            state = state + factor * g[at + h * HEAD : at + (h + 1) * HEAD, :].astype(f32)
        for z in range(s.shape[0]):
            out[z, rows, :] = state.astype(bf16)
            state = state * dec[h, z] + s[z, rows, :].astype(f32)


def mix_body(inside, q0, q1, q2, q3, prefix, rel_col, gain, m0, m1, m2, m3, rows_out, squares):
    qs, outs = (q0, q1, q2, q3), (m0, m1, m2, m3)
    length, block = rel_col.shape[1], q0.shape[0]
    picked = length // 8
    step, steps = pl.program_id(0), pl.num_programs(0)
    width = inside.shape[1]
    from_start = jnp.exp(rel_col[0])
    row = lax.broadcasted_iota(jnp.int32, (picked, length), 0)
    col = lax.broadcasted_iota(jnp.int32, (picked, length), 1)
    pick = (col == row * 8).astype(f32).astype(bf16)

    @pl.when(step == 0)
    def _():
        squares[...] = jnp.zeros_like(squares)

    for h in range(rel_col.shape[2]):
        cols = slice(h * HEAD, (h + 1) * HEAD)
        outside = dot(
            queries_of(qs, h),
            prefix[h // 2, (h % 2) * HEAD : (h % 2 + 1) * HEAD, :],
            ((1,), (0,)),
        )
        mixed = (inside[:, cols] + from_start[:, h : h + 1] * outside).astype(bf16)
        for d in range(4):
            outs[d][:, cols] = mixed[d * block : (d + 1) * block]
        rows = dot(pick, mixed, ((1,), (0,)))
        squares[...] += rows * rows
        at = pl.multiple_of(step * width + h * HEAD, HEAD)
        rows_out[:, pl.ds(at, HEAD)] = (rows * gain[:, cols]).astype(bf16)

    @pl.when(step == steps - 1)
    def _():
        total = jnp.sum(squares[...], axis=1, keepdims=True)
        high = total.astype(bf16).astype(f32)
        lane = lax.broadcasted_iota(jnp.int32, (picked, HEAD), 1)
        extra = jnp.where(lane == 0, high, jnp.where(lane == 1, total - high, 0.0))
        rows_out[:, rows_out.shape[1] - HEAD :] = extra.astype(bf16)


def project_body(r0, r1, weight, p0, p1, p2, p3):
    outs = (p0, p1, p2, p3)
    features, width = weight.shape
    for half, r in enumerate((r0, r1)):
        terms = dot(r[:, :features], weight[...], ((1,), (0,)))
        terms = terms.reshape(4, 4, 8, width)
        extra = r[:, features:].astype(f32).reshape(4, 4, 8, HEAD)
        for d in range(4):
            at = slice(half * 32, (half + 1) * 32)
            outs[d][at, :width] = terms[:, d].reshape(32, width).astype(bf16)
            outs[d][at, width:] = extra[:, d].reshape(32, HEAD).astype(bf16)


def dispatch_body(p0, p1, p2, p3, slots, out, *, features):
    width = out.shape[2]
    total = (p0[...].astype(f32) + p1[...].astype(f32)) + (p2[...].astype(f32) + p3[...].astype(f32))
    squares = total[:, width : width + 1] + total[:, width + 1 : width + 2]
    scale = lax.rsqrt(squares * (1.0 / features) + EPS)
    moe_in = (total[:, :width] * scale).astype(bf16)
    per = out.shape[1]
    count = (out.shape[0] // 2) * per
    target = lax.broadcasted_iota(jnp.int32, (count, total.shape[0]), 0)
    chosen = (target == slots[0:1, :]) | (target == slots[1:2, :])
    sent = dot(chosen.astype(f32).astype(bf16), moe_in, ((1,), (0,))).astype(bf16)
    for e in range(out.shape[0] // 2):
        block = sent[e * per : (e + 1) * per]
        out[2 * e] = block
        out[2 * e + 1] = block


def up_body(ids, own, other, w0, w1, w2, w3, *outs):
    width = own.shape[1]
    mine = pl.ds(pl.multiple_of(ids[2] * width, HEAD), width)
    rest = pl.ds(pl.multiple_of((1 - ids[2]) * width, HEAD), width)
    for w, out in zip((w0, w1, w2, w3), outs):
        part = dot(w[:, mine], own[...], ((1,), (1,)))
        part = part + dot(w[:, rest], other[...], ((1,), (1,)))
        out[...] = part.astype(bf16)


def down_body(ids, h0, h1, h2, h3, w0, w1, w2, w3, keep, send):
    width = keep.shape[1]
    mine = pl.ds(pl.multiple_of(ids[2] * width, HEAD), width)
    rest = pl.ds(pl.multiple_of((1 - ids[2]) * width, HEAD), width)
    hs, ws = (h0, h1, h2, h3), (w0, w1, w2, w3)
    send[...] = sum(dot(h[...], w[:, rest], ((0,), (0,))) for h, w in zip(hs, ws)).astype(bf16)
    keep[...] = sum(dot(h[...], w[:, mine], ((0,), (0,))) for h, w in zip(hs, ws))


def combine_body(ids, back, table, out):
    count = back.shape[0]
    lane = lax.broadcasted_iota(jnp.int32, (table.shape[0], count), 1)
    slot = ((lane >> 5) * 16 + (lane & 15)).astype(f32)
    gate = jnp.where(slot == table[:, 0:1], table[:, 2:3], 0.0) + jnp.where(
        slot == table[:, 1:2], table[:, 3:4], 0.0
    )
    high = gate.astype(bf16)
    low = (gate - high.astype(f32)).astype(bf16)
    total = dot(high, back[...], ((1,), (0,))) + dot(low, back[...], ((1,), (0,)))
    for r in range(2):
        for d in range(4):
            seg = lax.rem(ids[1] + 4 - d, 4) * 2 + ((ids[2] + r) & 1)
            at = (r * 4 + d) * 8
            out[seg] = total[at : at + 8].astype(bf16)


def norm_body(ids, m0, m1, m2, m3, gain, out):
    pieces = (m0, m1, m2, m3)
    width = m0.shape[1]
    total = jnp.zeros((m0.shape[0], 1), f32)
    for m in pieces:
        as_float = m[...].astype(f32)
        total = total + jnp.sum(as_float * as_float, axis=1, keepdims=True)
    scale = lax.rsqrt(total * (1.0 / (4 * width)) + EPS)
    for d, m in enumerate(pieces):
        at = lax.rem(ids[0] + d, 4) * PAIR
        for g in range(width // PAIR):
            cols = pl.ds(pl.multiple_of(at + g * 4 * PAIR, PAIR), PAIR)
            values = m[:, g * PAIR : (g + 1) * PAIR].astype(f32)
            out[:, cols] = (values * scale * gain[:, cols]).astype(bf16)


def over_seg(v):
    mine = jnp.concatenate([v] + [shifted(v, "y", d) for d in range(1, 4)], axis=0)
    return mine, shifted(mine, "c", 1)


def in_three(v):
    high = lax.reduce_precision(v, 8, 7)
    middle = lax.reduce_precision(v - high, 8, 7)
    return high, middle, lax.reduce_precision(v - high - middle, 8, 7)


def slot_ids(experts, expert_count):
    flat = experts.reshape(-1)
    onehot = (flat[:, None] == jnp.arange(expert_count, dtype=jnp.int32)[None, :]).astype(jnp.int32)
    earlier = flat[:, None] == flat[None, :]
    before = jnp.arange(flat.size)[:, None] > jnp.arange(flat.size)[None, :]
    position = jnp.sum((earlier & before).astype(jnp.int32), axis=1)
    return flat.reshape(experts.shape), position.reshape(experts.shape)


def on_device(
    queries, keys, values, log_decay, out_gain, out_proj, experts, gates, up_weight, down_weight
):
    x, y, c = lax.axis_index("x"), lax.axis_index("y"), lax.axis_index("c")
    ids = jnp.stack([x, y, c]).astype(jnp.int32)
    tokens, all_features = queries.shape
    features = all_features // 4
    heads = features // HEAD
    length = 4 * tokens
    n_z = lax.axis_size("z")
    model_slice = out_proj.shape[1]
    rows_dev = experts.shape[0]
    expert_count = 4 * n_z // 2

    def over_x(pieces):
        return [pieces[0]] + [shifted(pieces[d], "x", d) for d in range(1, 4)]

    kv_out = kernel_call(
        pack_pair_body, [struct((2, tokens, features), bf16)] * 4, (ids, keys, values), scalars=1
    )
    kv_out = list(kv_out)
    kv = over_x(kv_out)
    queries, kv[1] = lax.optimization_barrier((queries, kv[1]))
    q_out = kernel_call(pack_body, [struct((tokens, features), bf16)] * 4, (ids, queries), scalars=1)

    weight_out = lax.all_gather(out_proj, "z", axis=0, tiled=True)

    def sliced(w):
        quarter = w.shape[1] // 4
        return [
            lax.dynamic_slice_in_dim(w, ((y + d) % 4) * quarter, quarter, 1) for d in range(4)
        ]

    def over_y(pieces):
        return [pieces[0]] + [shifted(pieces[d], "y", d) for d in range(1, 4)]

    up = sliced(up_weight[0].T)
    kv[0], log_decay, *up = lax.optimization_barrier((kv_out[0], log_decay, *up))
    up = over_y(up)

    decay = log_decay.T.reshape(2 * n_z, length)
    upto = (
        jnp.arange(length, dtype=jnp.int32)[:, None] <= jnp.arange(length, dtype=jnp.int32)[None, :]
    ).astype(f32)
    rel_own = jnp.dot(decay, upto, precision=lax.Precision.HIGHEST).reshape(2, n_z, length)
    chunk_total = rel_own[:, :, -1]
    chunk_decay = jnp.exp(chunk_total)
    rel = lax.all_to_all(rel_own.transpose(1, 0, 2), "z", 0, 0, tiled=True).reshape(heads, length)
    by_source = rel.reshape(heads, 4, tokens)
    order = (x + 4 - jnp.arange(4, dtype=jnp.int32)) % 4
    rel_row = jnp.concatenate(
        [lax.dynamic_index_in_dim(by_source, order[d], 1, keepdims=False) for d in range(4)], axis=1
    )
    steps = 4
    rel_row = rel_row.reshape(steps, heads // steps, length)
    rel_col = rel_row.transpose(0, 2, 1)
    tot_row = rel[:, -1].reshape(steps, 1, heads // steps)

    expert, position = slot_ids(experts, expert_count)
    group_total = jnp.repeat(jnp.stack(in_three(jnp.sum(chunk_total, axis=1)), 1).reshape(6, 1), 128, 1)
    columns = [expert.astype(f32), position.astype(f32), *in_three(gates)]
    info = jnp.concatenate(columns + [jnp.zeros((rows_dev, 128 - 2 * len(columns)), f32)], axis=1)
    info = jnp.concatenate([info, group_total, jnp.zeros((2, 128), f32)], axis=0).astype(bf16)

    states = kernel_call(
        chunk_state_body,
        [struct((n_z, PAIR, HEAD), bf16)],
        (*kv, rel_col, tot_row),
        flops=2 * length * features * HEAD,
        steps=steps,
        blocks=(2, 2, 2, 2, 0, 0, 0),
    )[0]
    states, weight_out, *rest = lax.optimization_barrier(
        (states, weight_out, *q_out, *sliced(down_weight[0]))
    )
    q = over_x(rest[:4])
    down = over_y(rest[4:])
    states = lax.all_to_all(states, "z", 0, 0, tiled=True)
    states, *rest = lax.optimization_barrier((states, *up, *q))
    up, q = rest[:4], rest[4:]
    local = kernel_call(
        group_state_body, [struct((PAIR + 16, HEAD), bf16)], (chunk_decay, states, info), scalars=1
    )[0]
    groups = over_seg(local)
    inside = kernel_call(
        inside_body,
        [struct((length, features), f32)],
        (ids, *q, *kv, rel_col, rel_row),
        scalars=1,
        flops=4 * length * length * features,
        steps=steps,
        blocks=(1,) * 4 + (2,) * 4 + (0, 0, 1),
    )[0]
    prefix = kernel_call(
        prefix_body,
        [struct((n_z, PAIR, HEAD), bf16)],
        (ids, chunk_decay, states, *groups),
        scalars=2,
    )[0]
    prefix = lax.all_to_all(prefix, "z", 0, 0, tiled=True)
    info = jnp.concatenate(
        [g.reshape(4, PAIR + 16, HEAD)[:, PAIR : PAIR + rows_dev] for g in groups], axis=0
    ).astype(f32)
    slot = jnp.arange(8, dtype=jnp.int32)
    group = ((y + 4 - slot % 4) % 4) * 2 + (c + slot // 4) % 2
    slots = info[..., 0:2] * 16.0 + group[:, None, None].astype(f32) * 2.0 + info[..., 2:4]
    slots = slots.reshape(8 * rows_dev, 2)
    gate = (info[..., 4:6] + info[..., 6:8] + info[..., 8:10]).reshape(8 * rows_dev, 2)
    slot_rows = slots.T.astype(jnp.int32)
    combine_table = jnp.concatenate([slots, gate, jnp.zeros((8 * rows_dev, 124), f32)], axis=1)
    gain_own = lax.dynamic_index_in_dim(
        out_gain.reshape(n_z, 4, PAIR), x, 1, keepdims=False
    ).reshape(1, features)
    *mixed, rows, _ = kernel_call(
        mix_body,
        [struct((tokens, features), bf16)] * 4
        + [struct((length // 8, features + HEAD), bf16), struct((length // 8, HEAD), f32)],
        (inside, *q, prefix, rel_col, gain_own),
        flops=2 * length * features * HEAD,
        steps=steps,
        blocks=(1,) * 5 + (0, 0, 1) + (1,) * 4 + (None, None),
    )

    rows, down[2] = lax.optimization_barrier((rows, down[2]))

    terms = kernel_call(
        project_body,
        [struct((8 * rows_dev, model_slice + HEAD), bf16)] * 4,
        (*over_seg(rows), weight_out),
        flops=2 * length * features * model_slice,
    )
    terms = [terms[0]] + [shifted(terms[d], "x", -d) for d in range(1, 4)]
    outgoing = kernel_call(
        lambda *refs: dispatch_body(*refs, features=all_features),
        [struct((2 * expert_count, 16, model_slice), bf16)],
        (*terms, slot_rows),
    )[0]
    arrived = lax.all_to_all(outgoing, EP, 0, 0, tiled=True).reshape(-1, model_slice)
    arrived, down[1], down[3], combine_table = lax.optimization_barrier(
        (arrived, down[1], down[3], combine_table)
    )

    hidden_dev = up[0].shape[0]
    parts = kernel_call(
        up_body,
        [struct((hidden_dev, arrived.shape[0]), bf16)] * 4,
        (ids, arrived, shifted(arrived, "c", 1), *up),
        scalars=1,
        flops=16 * arrived.size * hidden_dev,
    )
    parts = [parts[0]] + [shifted(parts[d], "y", -d) for d in range(1, 4)]
    hidden = jax.nn.silu(sum(p.astype(f32) for p in parts)).astype(bf16)
    mixed = [mixed[0]] + [shifted(mixed[d], "x", -d) for d in range(1, 4)]
    hiddens = [hidden] + [shifted(hidden, "y", d) for d in range(1, 4)]
    keep, send = kernel_call(
        down_body,
        [struct(arrived.shape, f32), struct(arrived.shape, bf16)],
        (ids, *hiddens, *down),
        scalars=1,
        flops=16 * arrived.size * hidden_dev,
    )
    result = (keep + shifted(send, "c", 1).astype(f32)).astype(bf16)
    back = lax.all_to_all(
        result.reshape(outgoing.shape), EP, 0, 0, tiled=True
    ).reshape(-1, model_slice)
    mine = kernel_call(
        combine_body,
        [struct((8, rows_dev, model_slice), bf16)],
        (ids, back, combine_table),
        scalars=1,
    )[0]
    moe_out = lax.all_to_all(mine, SEG, 0, 0, tiled=True).transpose(1, 0, 2).reshape(rows_dev, -1)

    attn_out = kernel_call(
        norm_body,
        [struct((tokens, all_features), bf16)],
        (ids, *mixed, out_gain.reshape(1, -1)),
        scalars=1,
    )[0]
    return attn_out, moe_out


def solution(mesh):
    torus = Mesh(mesh.devices.reshape(4, 2, 8, 4), SEG_EP)
    placed = (
        P(SEG_EP, None),
        P(SEG_EP, None),
        P(SEG_EP, None),
        P(SEG, EP),
        P(),
        P(EP, SEG),
        P(SEG_EP, None),
        P(SEG_EP, None),
        P(EP, None, SEG),
        P(EP, SEG, None),
    )
    return jax.shard_map(
        on_device,
        mesh=torus,
        in_specs=placed,
        out_specs=(P(SEG_EP, None), P(SEG_EP, None)),
        check_vma=False,
    )
```

```python
import jax
import jax.numpy as jnp
from jax import lax
from jax.experimental import pallas as pl
from jax.experimental.pallas import tpu as pltpu
from jax.sharding import Mesh
from jax.sharding import PartitionSpec as P

SEG = ("y", "c")
EP = ("z", "x")
SEG_EP = SEG + EP

HEAD = 128
PAIR = 2 * HEAD
EPS = 1e-06
bf16 = jnp.bfloat16
f32 = jnp.float32


def shifted(v, axis, by):
    n = lax.axis_size(axis)
    return lax.ppermute(v, axis, [(i, (i + by) % n) for i in range(n)])


def in_hbm(a):
    return pltpu.with_memory_space_constraint(a, pltpu.HBM)


def kernel_call(body, outs, args, scalars=0, flops=0, steps=None, blocks=None):
    moved = sum(a.size * a.dtype.itemsize for a in list(args) + list(outs))
    tables = [pl.BlockSpec(memory_space=pltpu.SMEM) for _ in range(scalars)]
    arrays = list(args[scalars:]) + list(outs)
    if steps is None:
        specs = [pl.BlockSpec(memory_space=pltpu.VMEM) for _ in arrays]
    else:
        specs = []
        for a, dim in zip(arrays, blocks):
            shape = tuple(n // steps if i == dim else n for i, n in enumerate(a.shape))
            index = lambda i, dim=dim, rank=len(shape): tuple(i if j == dim else 0 for j in range(rank))
            specs.append(pl.BlockSpec(shape, index))
    inputs = len(args) - scalars
    if steps is not None:
        args = [
            in_hbm(a)
            if i >= scalars and a.dtype == bf16 and a.size >= 1 << 17
            else a
            for i, a in enumerate(args)
        ]
    return pl.pallas_call(
        body,
        out_shape=tuple(outs),
        grid=() if steps is None else (steps,),
        in_specs=tables + specs[:inputs],
        out_specs=tuple(specs[inputs:]),
        compiler_params=pltpu.CompilerParams(vmem_limit_bytes=2 * moved + (8 << 20)),
        cost_estimate=pl.CostEstimate(flops=flops, transcendentals=0, bytes_accessed=moved),
    )(*args)


def struct(shape, dtype):
    return jax.ShapeDtypeStruct(shape, dtype)


def dot(a, b, dims):
    return lax.dot_general(a, b, (dims, ((), ())), preferred_element_type=f32)


def pack_pair_body(ids, k, v, *outs):
    groups = k.shape[1] // (4 * PAIR)
    for d in range(4):
        at = lax.rem(ids[0] + d, 4) * PAIR
        for g in range(groups):
            cols = pl.ds(pl.multiple_of(at + g * 4 * PAIR, PAIR), PAIR)
            outs[d][0, :, g * PAIR : (g + 1) * PAIR] = k[:, cols]
            outs[d][1, :, g * PAIR : (g + 1) * PAIR] = v[:, cols]


def pack_body(ids, q, *outs):
    groups = q.shape[1] // (4 * PAIR)
    for d in range(4):
        at = lax.rem(ids[0] + d, 4) * PAIR
        for g in range(groups):
            cols = pl.ds(pl.multiple_of(at + g * 4 * PAIR, PAIR), PAIR)
            outs[d][:, g * PAIR : (g + 1) * PAIR] = q[:, cols]


def queries_of(pieces, h):
    return jnp.concatenate([p[:, h * HEAD : (h + 1) * HEAD] for p in pieces], axis=0)


def rows_of(pieces, lead, h):
    cols = slice(h * HEAD, (h + 1) * HEAD)
    return jnp.concatenate([p[lead, :, cols] for p in pieces], axis=0)


def chunk_state_body(kv0, kv1, kv2, kv3, rel_col, tot_row, out):
    pieces = (kv0, kv1, kv2, kv3)
    to_end = jnp.exp(tot_row[0] - rel_col[0])
    for h in range(rel_col.shape[2]):
        k = rows_of(pieces, 0, h).astype(f32)
        weighted = (k * to_end[:, h : h + 1]).astype(bf16)
        state = dot(weighted, rows_of(pieces, 1, h), ((0,), (0,)))
        out[h // 2, (h % 2) * HEAD : (h % 2 + 1) * HEAD, :] = state.astype(bf16)


def inside_body(ids, q0, q1, q2, q3, kv0, kv1, kv2, kv3, rel_col, rel_row, out):
    qs, kvs = (q0, q1, q2, q3), (kv0, kv1, kv2, kv3)
    length, block = rel_col.shape[1], q0.shape[0]

    def positions(axis):
        i = lax.broadcasted_iota(jnp.int32, (length, length), axis)
        return ((ids[0] + 4 - i // block) & 3) * block + (i & (block - 1))

    causal = positions(0) >= positions(1)
    for h in range(rel_col.shape[2]):
        gap = rel_col[0, :, h : h + 1] - rel_row[0, h : h + 1, :]
        weight = jnp.exp(jnp.where(causal, gap, -jnp.inf))
        scores = dot(queries_of(qs, h), rows_of(kvs, 0, h), ((1,), (1,)))
        mixing = (scores * weight).astype(bf16)
        out[:, h * HEAD : (h + 1) * HEAD] = dot(mixing, rows_of(kvs, 1, h), ((1,), (0,)))


def group_state_body(dec, s, info, out):
    for h in range(2):
        rows = slice(h * HEAD, (h + 1) * HEAD)
        total = s[0, rows, :].astype(f32)
        for z in range(1, s.shape[0]):
            total = total * dec[h, z] + s[z, rows, :].astype(f32)
        out[rows, :] = total.astype(bf16)
    out[PAIR:, :] = info[...]


def prefix_body(ids, dec, s, g0, g1, out):
    own = ids[1] * 2 + ids[2]
    each = g0.shape[0] // 4
    slots = [(g, d * each, r) for r, g in enumerate((g0, g1)) for d in range(4)]
    group = [
        lax.rem(ids[1] + 4 - d, 4) * 2 + ((ids[2] + r) & 1) for r in range(2) for d in range(4)
    ]
    for h in range(2):
        rows = slice(h * HEAD, (h + 1) * HEAD)

        def ending(slot):
            g, at, _ = slots[slot]
            first = at + PAIR + 8 + 3 * h
            e = [g[first + k : first + k + 1, :].astype(f32) for k in range(3)]
            return (e[0] + e[1]) + e[2]

        ends = [ending(slot) for slot in range(8)]
        state = jnp.zeros((HEAD, HEAD), f32)
        for i, (g, at, _) in enumerate(slots):
            gap = jnp.zeros((1, HEAD), f32)
            for j in range(8):
                between = (group[i] < group[j]) & (group[j] < own)
                gap = gap + jnp.where(between, 1.0, 0.0) * ends[j]
            factor = jnp.where(group[i] < own, 1.0, 0.0) * jnp.exp(gap)
            state = state + factor * g[at + h * HEAD : at + (h + 1) * HEAD, :].astype(f32)
        for z in range(s.shape[0]):
            out[z, rows, :] = state.astype(bf16)
            state = state * dec[h, z] + s[z, rows, :].astype(f32)


def mix_body(inside, q0, q1, q2, q3, prefix, rel_col, gain, m0, m1, m2, m3, rows_out, squares):
    qs, outs = (q0, q1, q2, q3), (m0, m1, m2, m3)
    length, block = rel_col.shape[1], q0.shape[0]
    picked = length // 8
    step, steps = pl.program_id(0), pl.num_programs(0)
    width = inside.shape[1]
    from_start = jnp.exp(rel_col[0])
    row = lax.broadcasted_iota(jnp.int32, (picked, length), 0)
    col = lax.broadcasted_iota(jnp.int32, (picked, length), 1)
    pick = (col == row * 8).astype(f32).astype(bf16)

    @pl.when(step == 0)
    def _():
        squares[...] = jnp.zeros_like(squares)

    for h in range(rel_col.shape[2]):
        cols = slice(h * HEAD, (h + 1) * HEAD)
        outside = dot(
            queries_of(qs, h),
            prefix[h // 2, (h % 2) * HEAD : (h % 2 + 1) * HEAD, :],
            ((1,), (0,)),
        )
        mixed = (inside[:, cols] + from_start[:, h : h + 1] * outside).astype(bf16)
        for d in range(4):
            outs[d][:, cols] = mixed[d * block : (d + 1) * block]
        rows = dot(pick, mixed, ((1,), (0,)))
        squares[...] += rows * rows
        at = pl.multiple_of(step * width + h * HEAD, HEAD)
        rows_out[:, pl.ds(at, HEAD)] = (rows * gain[:, cols]).astype(bf16)

    @pl.when(step == steps - 1)
    def _():
        total = jnp.sum(squares[...], axis=1, keepdims=True)
        high = total.astype(bf16).astype(f32)
        lane = lax.broadcasted_iota(jnp.int32, (picked, HEAD), 1)
        extra = jnp.where(lane == 0, high, jnp.where(lane == 1, total - high, 0.0))
        rows_out[:, rows_out.shape[1] - HEAD :] = extra.astype(bf16)


def project_body(r0, r1, weight, p0, p1, p2, p3):
    outs = (p0, p1, p2, p3)
    features, width = weight.shape
    for half, r in enumerate((r0, r1)):
        terms = dot(r[:, :features], weight[...], ((1,), (0,)))
        terms = terms.reshape(4, 4, 8, width)
        extra = r[:, features:].astype(f32).reshape(4, 4, 8, HEAD)
        for d in range(4):
            at = slice(half * 32, (half + 1) * 32)
            outs[d][at, :width] = terms[:, d].reshape(32, width).astype(bf16)
            outs[d][at, width:] = extra[:, d].reshape(32, HEAD).astype(bf16)


def dispatch_body(p0, p1, p2, p3, slots, out, *, features):
    width = out.shape[2]
    total = (p0[...].astype(f32) + p1[...].astype(f32)) + (p2[...].astype(f32) + p3[...].astype(f32))
    squares = total[:, width : width + 1] + total[:, width + 1 : width + 2]
    scale = lax.rsqrt(squares * (1.0 / features) + EPS)
    moe_in = (total[:, :width] * scale).astype(bf16)
    per = out.shape[1]
    count = (out.shape[0] // 2) * per
    target = lax.broadcasted_iota(jnp.int32, (count, total.shape[0]), 0)
    chosen = (target == slots[0:1, :]) | (target == slots[1:2, :])
    sent = dot(chosen.astype(f32).astype(bf16), moe_in, ((1,), (0,))).astype(bf16)
    for e in range(out.shape[0] // 2):
        block = sent[e * per : (e + 1) * per]
        out[2 * e] = block
        out[2 * e + 1] = block


def up_body(ids, own, other, w0, w1, w2, w3, *outs):
    width = own.shape[1]
    mine = pl.ds(pl.multiple_of(ids[2] * width, HEAD), width)
    rest = pl.ds(pl.multiple_of((1 - ids[2]) * width, HEAD), width)
    for w, out in zip((w0, w1, w2, w3), outs):
        part = dot(w[:, mine], own[...], ((1,), (1,)))
        part = part + dot(w[:, rest], other[...], ((1,), (1,)))
        out[...] = part.astype(bf16)


def down_body(ids, h0, h1, h2, h3, w0, w1, w2, w3, out, *, other):
    width = out.shape[1]
    part = 1 - ids[2] if other else ids[2]
    cols = pl.ds(pl.multiple_of(part * width, HEAD), width)
    hs, ws = (h0, h1, h2, h3), (w0, w1, w2, w3)
    out[...] = sum(dot(h[...], w[:, cols], ((0,), (0,))) for h, w in zip(hs, ws)).astype(out.dtype)


def combine_body(ids, back, table, out):
    count = back.shape[0]
    lane = lax.broadcasted_iota(jnp.int32, (table.shape[0], count), 1)
    slot = ((lane >> 5) * 16 + (lane & 15)).astype(f32)
    gate = jnp.where(slot == table[:, 0:1], table[:, 2:3], 0.0) + jnp.where(
        slot == table[:, 1:2], table[:, 3:4], 0.0
    )
    high = gate.astype(bf16)
    low = (gate - high.astype(f32)).astype(bf16)
    total = dot(high, back[...], ((1,), (0,))) + dot(low, back[...], ((1,), (0,)))
    for r in range(2):
        for d in range(4):
            seg = lax.rem(ids[1] + 4 - d, 4) * 2 + ((ids[2] + r) & 1)
            at = (r * 4 + d) * 8
            out[seg] = total[at : at + 8].astype(bf16)


def norm_body(ids, m0, m1, m2, m3, gain, out):
    pieces = (m0, m1, m2, m3)
    width = m0.shape[1]
    total = jnp.zeros((m0.shape[0], 1), f32)
    for m in pieces:
        as_float = m[...].astype(f32)
        total = total + jnp.sum(as_float * as_float, axis=1, keepdims=True)
    scale = lax.rsqrt(total * (1.0 / (4 * width)) + EPS)
    for d, m in enumerate(pieces):
        at = lax.rem(ids[0] + d, 4) * PAIR
        for g in range(width // PAIR):
            cols = pl.ds(pl.multiple_of(at + g * 4 * PAIR, PAIR), PAIR)
            values = m[:, g * PAIR : (g + 1) * PAIR].astype(f32)
            out[:, cols] = (values * scale * gain[:, cols]).astype(bf16)


def over_seg(v):
    mine = jnp.concatenate([v] + [shifted(v, "y", d) for d in range(1, 4)], axis=0)
    return mine, shifted(mine, "c", 1)


def in_three(v):
    high = lax.reduce_precision(v, 8, 7)
    middle = lax.reduce_precision(v - high, 8, 7)
    return high, middle, lax.reduce_precision(v - high - middle, 8, 7)


def slot_ids(experts, expert_count):
    flat = experts.reshape(-1)
    onehot = (flat[:, None] == jnp.arange(expert_count, dtype=jnp.int32)[None, :]).astype(jnp.int32)
    earlier = flat[:, None] == flat[None, :]
    before = jnp.arange(flat.size)[:, None] > jnp.arange(flat.size)[None, :]
    position = jnp.sum((earlier & before).astype(jnp.int32), axis=1)
    return flat.reshape(experts.shape), position.reshape(experts.shape)


def on_device(
    queries, keys, values, log_decay, out_gain, out_proj, experts, gates, up_weight, down_weight
):
    x, y, c = lax.axis_index("x"), lax.axis_index("y"), lax.axis_index("c")
    ids = jnp.stack([x, y, c]).astype(jnp.int32)
    tokens, all_features = queries.shape
    features = all_features // 4
    heads = features // HEAD
    length = 4 * tokens
    n_z = lax.axis_size("z")
    model_slice = out_proj.shape[1]
    rows_dev = experts.shape[0]
    expert_count = 4 * n_z // 2

    def over_x(pieces):
        return [pieces[0]] + [shifted(pieces[d], "x", d) for d in range(1, 4)]

    kv_out = kernel_call(
        pack_pair_body, [struct((2, tokens, features), bf16)] * 4, (ids, keys, values), scalars=1
    )
    kv_out = list(kv_out)
    kv = over_x(kv_out)
    q_out = kernel_call(pack_body, [struct((tokens, features), bf16)] * 4, (ids, queries), scalars=1)

    weight_out = lax.all_gather(out_proj, "z", axis=0, tiled=True)

    def sliced(w):
        quarter = w.shape[1] // 4
        return [
            lax.dynamic_slice_in_dim(w, ((y + d) % 4) * quarter, quarter, 1) for d in range(4)
        ]

    def over_y(pieces):
        return [pieces[0]] + [shifted(pieces[d], "y", d) for d in range(1, 4)]

    up = sliced(up_weight[0].T)
    kv[0], log_decay = lax.optimization_barrier((kv_out[0], log_decay))
    up = over_y(up)

    decay = log_decay.T.reshape(2 * n_z, length)
    upto = (
        jnp.arange(length, dtype=jnp.int32)[:, None] <= jnp.arange(length, dtype=jnp.int32)[None, :]
    ).astype(f32)
    rel_own = jnp.dot(decay, upto, precision=lax.Precision.HIGHEST).reshape(2, n_z, length)
    chunk_total = rel_own[:, :, -1]
    chunk_decay = jnp.exp(chunk_total)
    rel = lax.all_to_all(rel_own.transpose(1, 0, 2), "z", 0, 0, tiled=True).reshape(heads, length)
    by_source = rel.reshape(heads, 4, tokens)
    order = (x + 4 - jnp.arange(4, dtype=jnp.int32)) % 4
    rel_row = jnp.concatenate(
        [lax.dynamic_index_in_dim(by_source, order[d], 1, keepdims=False) for d in range(4)], axis=1
    )
    steps = 4
    rel_row = rel_row.reshape(steps, heads // steps, length)
    rel_col = rel_row.transpose(0, 2, 1)
    tot_row = rel[:, -1].reshape(steps, 1, heads // steps)

    expert, position = slot_ids(experts, expert_count)
    group_total = jnp.repeat(jnp.stack(in_three(jnp.sum(chunk_total, axis=1)), 1).reshape(6, 1), 128, 1)
    columns = [expert.astype(f32), position.astype(f32), *in_three(gates)]
    info = jnp.concatenate(columns + [jnp.zeros((rows_dev, 128 - 2 * len(columns)), f32)], axis=1)
    info = jnp.concatenate([info, group_total, jnp.zeros((2, 128), f32)], axis=0).astype(bf16)

    states = kernel_call(
        chunk_state_body,
        [struct((n_z, PAIR, HEAD), bf16)],
        (*kv, rel_col, tot_row),
        flops=2 * length * features * HEAD,
        steps=steps,
        blocks=(2, 2, 2, 2, 0, 0, 0),
    )[0]
    states, weight_out, *rest = lax.optimization_barrier(
        (states, weight_out, *q_out, *sliced(down_weight[0]))
    )
    q = over_x(rest[:4])
    down = over_y(rest[4:])
    states = lax.all_to_all(states, "z", 0, 0, tiled=True)
    states, *rest = lax.optimization_barrier((states, *up, *q))
    up, q = rest[:4], rest[4:]
    local = kernel_call(
        group_state_body, [struct((PAIR + 16, HEAD), bf16)], (chunk_decay, states, info), scalars=1
    )[0]
    groups = over_seg(local)
    inside = kernel_call(
        inside_body,
        [struct((length, features), f32)],
        (ids, *q, *kv, rel_col, rel_row),
        scalars=1,
        flops=4 * length * length * features,
        steps=steps,
        blocks=(1,) * 4 + (2,) * 4 + (0, 0, 1),
    )[0]
    prefix = kernel_call(
        prefix_body,
        [struct((n_z, PAIR, HEAD), bf16)],
        (ids, chunk_decay, states, *groups),
        scalars=2,
    )[0]
    prefix = lax.all_to_all(prefix, "z", 0, 0, tiled=True)
    info = jnp.concatenate(
        [g.reshape(4, PAIR + 16, HEAD)[:, PAIR : PAIR + rows_dev] for g in groups], axis=0
    ).astype(f32)
    slot = jnp.arange(8, dtype=jnp.int32)
    group = ((y + 4 - slot % 4) % 4) * 2 + (c + slot // 4) % 2
    slots = info[..., 0:2] * 16.0 + group[:, None, None].astype(f32) * 2.0 + info[..., 2:4]
    slots = slots.reshape(8 * rows_dev, 2)
    gate = (info[..., 4:6] + info[..., 6:8] + info[..., 8:10]).reshape(8 * rows_dev, 2)
    slot_rows = slots.T.astype(jnp.int32)
    combine_table = jnp.concatenate([slots, gate, jnp.zeros((8 * rows_dev, 124), f32)], axis=1)
    gain_own = lax.dynamic_index_in_dim(
        out_gain.reshape(n_z, 4, PAIR), x, 1, keepdims=False
    ).reshape(1, features)
    *mixed, rows, _ = kernel_call(
        mix_body,
        [struct((tokens, features), bf16)] * 4
        + [struct((length // 8, features + HEAD), bf16), struct((length // 8, HEAD), f32)],
        (inside, *q, prefix, rel_col, gain_own),
        flops=2 * length * features * HEAD,
        steps=steps,
        blocks=(1,) * 5 + (0, 0, 1) + (1,) * 4 + (None, None),
    )

    rows, down[2] = lax.optimization_barrier((rows, down[2]))

    terms = kernel_call(
        project_body,
        [struct((8 * rows_dev, model_slice + HEAD), bf16)] * 4,
        (*over_seg(rows), weight_out),
        flops=2 * length * features * model_slice,
    )
    terms = [terms[0]] + [shifted(terms[d], "x", -d) for d in range(1, 4)]
    outgoing = kernel_call(
        lambda *refs: dispatch_body(*refs, features=all_features),
        [struct((2 * expert_count, 16, model_slice), bf16)],
        (*terms, slot_rows),
    )[0]
    arrived = lax.all_to_all(outgoing, EP, 0, 0, tiled=True).reshape(-1, model_slice)
    arrived, down[1], down[3], combine_table = lax.optimization_barrier(
        (arrived, down[1], down[3], combine_table)
    )

    hidden_dev = up[0].shape[0]
    parts = kernel_call(
        up_body,
        [struct((hidden_dev, arrived.shape[0]), bf16)] * 4,
        (ids, arrived, shifted(arrived, "c", 1), *map(in_hbm, up)),
        scalars=1,
        flops=16 * arrived.size * hidden_dev,
    )
    parts = [parts[0]] + [shifted(parts[d], "y", -d) for d in range(1, 4)]
    hidden = jax.nn.silu(sum(p.astype(f32) for p in parts)).astype(bf16)
    mixed = [mixed[0]] + [shifted(mixed[d], "x", -d) for d in range(1, 4)]
    hiddens = [hidden] + [shifted(hidden, "y", d) for d in range(1, 4)]
    def down_half(other, dtype):
        return kernel_call(
            lambda *refs: down_body(*refs, other=other),
            [struct(arrived.shape, dtype)],
            (ids, *hiddens, *down),
            scalars=1,
            flops=8 * arrived.size * hidden_dev,
        )[0]

    send = down_half(True, bf16)
    keep = down_half(False, f32)
    result = (keep + shifted(send, "c", 1).astype(f32)).astype(bf16)
    back = lax.all_to_all(
        result.reshape(outgoing.shape), EP, 0, 0, tiled=True
    ).reshape(-1, model_slice)
    mine = kernel_call(
        combine_body,
        [struct((8, rows_dev, model_slice), bf16)],
        (ids, back, combine_table),
        scalars=1,
    )[0]
    moe_out = lax.all_to_all(mine, SEG, 0, 0, tiled=True).transpose(1, 0, 2).reshape(rows_dev, -1)

    attn_out = kernel_call(
        norm_body,
        [struct((tokens, all_features), bf16)],
        (ids, *mixed, out_gain.reshape(1, -1)),
        scalars=1,
    )[0]
    return attn_out, moe_out


def solution(mesh):
    torus = Mesh(mesh.devices.reshape(4, 2, 8, 4), SEG_EP)
    placed = (
        P(SEG_EP, None),
        P(SEG_EP, None),
        P(SEG_EP, None),
        P(SEG, EP),
        P(),
        P(EP, SEG),
        P(SEG_EP, None),
        P(SEG_EP, None),
        P(EP, None, SEG),
        P(EP, SEG, None),
    )
    return jax.shard_map(
        on_device,
        mesh=torus,
        in_specs=placed,
        out_specs=(P(SEG_EP, None), P(SEG_EP, None)),
        check_vma=False,
    )
```
